32 devices in a mesh: op: 16 (over z, x, core), term: 2 (over y).
Axes of the slice: x: 2, y: 2, z: 4, core: 2. Of those that a mesh axis runs over, the one named last changes fastest.
Arguments:
- wavefunction: float32 [16, 384, 384], P('op'), may hold values from -6 to 6
- left_dims: int32 [16], P('op'), may hold values from 192 to 384
- right_dims: int32 [16], P('op'), may hold values from 192 to 384
- left_operators: float32 [16, 2, 384, 384], P('op', 'term'), may hold values from -0.21875 to 0.21875
- right_operators: float32 [16, 2, 384, 384], P('op', 'term'), may hold values from -0.3125 to 0.3125
- charges: int32 [16, 2], P('op', 'term'), may hold values from 0 to 11
Outputs:
- applied: float32 [16, 384, 384], P('op', 'term')
The draws below stay inside these ranges and needn't reach their ends.
Inputs may be any that keep to these rules, and one draw needn't show every extreme that they name: `charges`: a term of source sector s acts into sector (s + charge) mod 16.
All inputs are finite; a program needn't handle non-finite values.
Results may differ from the reference program's by a relative error of at most 0.0003.
Values sent between devices are 32-bit elements; how exact they have to be, the bound alone decides.
No kernel may reach another device: no remote copies, remote signals or barrier semaphores. Data moves between devices by JAX's collectives and lax.ppermute only.
A program may use at most 64 MiB of HBM per device.

```python
import jax
import jax.numpy as jnp
from jax import lax

B = 384
CHARGES = 12
SECTORS = 16
TPT = 2


def place_ends(values, rng, smallest, top_value):
    dims = values.shape
    spot = [jax.random.randint(jax.random.fold_in(rng, axis), (), 0, dims[axis]) for axis in range(len(dims))]
    values = values.at[tuple(spot)].set(smallest)
    longest = dims.index(max(dims))
    spot[longest] = (spot[longest] + 1) % dims[longest]
    return values.at[tuple(spot)].set(top_value)


def level_of(key, dims, shards, least, top_value):
    loudness, own = 1.0, jax.random.fold_in(key, 6)
    for dim, parts in shards:
        draws = jnp.exp(jax.random.uniform(jax.random.fold_in(own, dim), (parts,), jnp.float32, least / len(shards), top_value / len(shards)))
        loudness = loudness * jnp.repeat(draws, dims[dim] // parts).reshape([-1 if axis == dim else 1 for axis in range(len(dims))])
    return loudness


def scatter_about(own_key, shape, deviation, most, split=(), kind=jnp.bfloat16):
    factor_of = level_of(own_key, shape, split, -0.22, 0.18) if split else 1.0
    array = jax.random.normal(own_key, shape, jnp.float32) * deviation * factor_of
    return jnp.minimum(jnp.maximum(array, -most), most).astype(kind)


def setup_inputs(seed: int = 0) -> dict:
    arg_keys = jax.random.split(jax.random.key(seed), 7)
    wavefunction = scatter_about(arg_keys[0], (SECTORS, B, B), 1.0, 6.0, ((0, 16),), jnp.float32)
    left_dims = place_ends(jax.random.randint(arg_keys[1], (SECTORS,), B // 2, B + 1), jax.random.fold_in(arg_keys[1], 1), B // 2, B).astype(jnp.int32)
    right_dims = place_ends(jax.random.randint(arg_keys[2], (SECTORS,), B // 2, B + 1), jax.random.fold_in(arg_keys[2], 1), B // 2, B).astype(jnp.int32)
    left_operators = scatter_about(arg_keys[3], (SECTORS, TPT, B, B), (B * TPT) ** -0.5, 0.21875, ((0, 16), (1, 2)), jnp.float32)
    right_operators = scatter_about(arg_keys[4], (SECTORS, TPT, B, B), B ** -0.5, 0.3125, ((0, 16), (1, 2)), jnp.float32)
    charges = place_ends(jax.random.randint(arg_keys[5], (SECTORS, TPT), 0, CHARGES), jax.random.fold_in(arg_keys[5], 1), 0, CHARGES - 1).astype(jnp.int32)
    return {"wavefunction": wavefunction, "left_dims": left_dims, "right_dims": right_dims, "left_operators": left_operators, "right_operators": right_operators, "charges": charges}


TOP_CHARGE = lax.Precision.HIGHEST


def reference(wavefunction, left_dims, right_dims, left_operators, right_operators, charges):
    positions = jnp.arange(B).astype(jnp.int32)
    live_mask = ((positions[None, :, None] < left_dims[:, None, None]) & (positions[None, None, :] < right_dims[:, None, None])).astype(jnp.float32)
    mask_applied = wavefunction * live_mask
    sectors = jnp.arange(SECTORS).astype(jnp.int32)

    def one_sector(carried, sector_items):
        incoming_block, left_term_stack, right_term_stack, term_charge, source = sector_items
        left_product = jnp.einsum("ims,sd->imd", left_term_stack, incoming_block, precision=TOP_CHARGE)
        term_contribution = jnp.einsum("opu,oru->opr", left_product, right_term_stack, precision=TOP_CHARGE)
        targets = (source + term_charge) % SECTORS
        one_hot = (sectors[:, None] == targets[None, :]).astype(jnp.float32)
        return carried + jnp.einsum("kt,tab->kab", one_hot, term_contribution, precision=TOP_CHARGE), source

    summed, unused = lax.scan(one_sector, jnp.zeros((SECTORS, B, B), jnp.float32), (mask_applied, left_operators, right_operators, charges, sectors))
    return summed * live_mask
```

```python
import functools

import jax
import jax.numpy as jnp
from jax import lax
from jax.experimental import pallas as pl
from jax.experimental.pallas import tpu as pltpu
from jax.sharding import PartitionSpec as P

CHARGES = 12
LANES = 128
TAG = 8
CORES = 2

SCALAR = pl.BlockSpec(memory_space=pltpu.SMEM)
WHOLE = pl.BlockSpec(memory_space=pltpu.VMEM)


def halves(value):
    high = value.astype(jnp.bfloat16)
    return high, (value - high.astype(jnp.float32)).astype(jnp.bfloat16)


def product(left, right, dims):
    def one(a, b):
        return lax.dot_general(a, b, (dims, ((), ())), preferred_element_type=jnp.float32)

    return one(left[0], right[0]) + (one(left[0], right[1]) + one(left[1], right[0]))


def contribution_kernel(terms, sectors, left_dim, right_dim, charge, place, wave, left, right, *items):
    order = wave.shape[1]
    rows = order // terms
    spot = lax.broadcasted_iota(jnp.int32, (order, order), 0)
    across = lax.broadcasted_iota(jnp.int32, (order, order), 1)
    live = (spot < left_dim[0]) & (across < right_dim[0])
    masked = jnp.where(live, wave[0], 0.0)
    inner = halves(product(halves(masked), halves(right[0, 0]), ((1,), (1,))))
    target = lax.rem(place[0] + charge[0, 0], sectors).astype(jnp.float32)
    for step in reversed(range(terms)):
        block = lax.rem(place[1] + step, terms)
        start = pl.multiple_of(block * rows, 8)
        part = product(halves(left[0, 0, pl.ds(start, rows), :]), inner, ((1,), (0,)))
        for col in range(order // LANES):
            items[step][col * rows : (col + 1) * rows, :] = part[:, col * LANES : (col + 1) * LANES]
        items[step][order // LANES * rows :, :] = jnp.full((TAG, LANES), target, jnp.float32)


def slots_kernel(count, body, stride, sectors, place, *refs):
    slots, items = refs[len(refs) - count :], refs[: len(refs) - count]
    lines = slots[0].shape[0]
    here = place[0]
    tags = [item[lines:, :] for item in items]
    wanted = [
        lax.rem(here + step * stride, sectors).astype(jnp.float32) for step in range(count)
    ]
    picks = [[tag == want for tag in tags] for want in wanted]

    @pl.loop(0, lines // TAG, unroll=4)
    def _(tile):
        at = pl.ds(pl.multiple_of(tile * TAG, TAG), TAG)
        values = [item[at, :] for item in items]
        for step in range(count):
            total = jnp.where(picks[step][0], values[0], 0.0)
            for pick, value in zip(picks[step][1:], values[1:]):
                total = total + jnp.where(pick, value, 0.0)
            slots[step][at, :] = total


def owned_kernel(left_dim, right_dim, place, *refs):
    out, parts = refs[-1], refs[:-1]
    rows, order = out.shape[1:]
    spot = place[1] * rows + lax.broadcasted_iota(jnp.int32, (rows, LANES), 0)
    across = lax.broadcasted_iota(jnp.int32, (rows, LANES), 1)
    for col in range(order // LANES):
        total = parts[0][col * rows : (col + 1) * rows, :]
        for part in parts[1:]:
            total = total + part[col * rows : (col + 1) * rows, :]
        live = (spot < left_dim[0]) & (across + col * LANES < right_dim[0])
        out[0, :, col * LANES : (col + 1) * LANES] = jnp.where(live, total, 0.0)


def on_device(sizes, wavefunction, left_dims, right_dims, left_operators, right_operators, charges):
    sectors, terms, deep, wide = sizes
    order = wavefunction.shape[1]
    rows = order // terms
    lines = order // LANES * rows
    layer = wide * CORES
    place = jnp.stack([lax.axis_index("op"), lax.axis_index("term")]).astype(jnp.int32)

    def shape(count):
        return jax.ShapeDtypeStruct((count, LANES), jnp.float32)

    def moved(value, dz, dx, dk):
        pairs = []
        for source in range(sectors):
            z, x, k = source // layer, source // CORES % wide, source % CORES
            z, x, k = (z + dz) % deep, (x + dx) % wide, (k + dk) % CORES
            pairs.append((source, (z * wide + x) * CORES + k))
        return lax.ppermute(value, "op", pairs)

    def across_terms(value, step):
        return lax.ppermute(value, "term", [(t, (t + step) % terms) for t in range(terms)])

    parts = pl.pallas_call(
        functools.partial(contribution_kernel, terms, sectors),
        out_shape=[shape(lines + TAG)] * terms,
        in_specs=[SCALAR] * 4 + [WHOLE] * 3,
        out_specs=[WHOLE] * terms,
        name="contribution",
    )(left_dims, right_dims, charges, place, wavefunction, left_operators, right_operators)
    own = [parts[0]] + [across_terms(parts[step], step) for step in range(1, terms)]
    plane = list(own)
    for step in range(1, wide):
        plane += [moved(item, 0, step, 0) for item in own]
    items = plane + [moved(item, 0, 0, 1) for item in plane]

    count = min(deep, (CHARGES - 1 + layer - 1) // layer + 1)
    slots = pl.pallas_call(
        functools.partial(slots_kernel, count, lines, layer, sectors),
        out_shape=[shape(lines)] * count,
        in_specs=[SCALAR] + [WHOLE] * len(items),
        out_specs=[WHOLE] * count,
        name="slots",
    )(place, *items)
    sums = [slots[0]] + [moved(slots[step], step, 0, 0) for step in range(1, count)]
    return pl.pallas_call(
        owned_kernel,
        out_shape=jax.ShapeDtypeStruct((1, rows, order), jnp.float32),
        in_specs=[SCALAR] * 3 + [WHOLE] * count,
        out_specs=WHOLE,
        name="owned",
    )(left_dims, right_dims, place, *sums)


def factors(sectors):
    chips = sectors // CORES
    deep = 1
    while deep * deep < chips:
        deep *= 2
    return deep, chips // deep


def solution(mesh):
    sectors, terms = mesh.shape["op"], mesh.shape["term"]
    in_specs = (
        P("op", None, None),
        P("op"),
        P("op"),
        P("op", "term", None, None),
        P("op", "term", None, None),
        P("op", "term"),
    )
    return jax.shard_map(
        functools.partial(on_device, (sectors, terms, *factors(sectors))),
        mesh=mesh,
        in_specs=in_specs,
        out_specs=P("op", "term", None),
        check_vma=False,
    )
```

```python
import functools

import jax
import jax.numpy as jnp
from jax import lax
from jax.experimental import pallas as pl
from jax.experimental.pallas import tpu as pltpu
from jax.sharding import PartitionSpec as P

CHARGES = 12
LANES = 128
TAG = 8
CORES = 2
PIECES = 2
VMEM = 24 * 2**20

HBM = pl.BlockSpec(memory_space=pltpu.HBM)
WHOLE = pl.BlockSpec(memory_space=pltpu.VMEM)


def small():
    return pltpu.CompilerParams(vmem_limit_bytes=VMEM)


def halves(value):
    high = value.astype(jnp.bfloat16)
    return high, (value - high.astype(jnp.float32)).astype(jnp.bfloat16)


def product(left, right, dims):
    def one(a, b):
        return lax.dot_general(a, b, (dims, ((), ())), preferred_element_type=jnp.float32)

    return one(left[0], right[0]) + (one(left[0], right[1]) + one(left[1], right[0]))


def contribution_kernel(terms, pieces, facts, wave, left, right, *refs):
    items = refs[: terms * pieces]
    wave_here, left_here, right_here, sems = refs[terms * pieces :]
    loads = [
        pltpu.make_async_copy(source, target, sems.at[index])
        for index, (source, target) in enumerate(
            (
                (wave.at[0], wave_here),
                (right.at[0, 0], right_here),
                (left.at[0, 0], left_here),
            )
        )
    ]
    for load in loads:
        load.start()
    loads[0].wait()
    loads[1].wait()
    order = wave_here.shape[1]
    rows = order // terms
    spot = lax.broadcasted_iota(jnp.int32, (order, LANES), 0)
    across = lax.broadcasted_iota(jnp.int32, (order, LANES), 1)
    live = jnp.concatenate(
        [
            (spot < facts[:1, :]) & (across + col < facts[TAG : TAG + 1, :])
            for col in range(0, order, LANES)
        ],
        axis=1,
    )
    masked = jnp.where(live, wave_here[...], 0.0)
    inner = halves(product(halves(masked), halves(right_here[...]), ((1,), (1,))))
    target = facts[2 * TAG :, :].astype(jnp.float32)
    loads[2].wait()
    part_rows = rows // pieces
    for step in reversed(range(terms)):
        block = lax.rem(lax.axis_index("term") + step, terms)
        start = pl.multiple_of(block * rows, 8)
        whole = product(halves(left_here[pl.ds(start, rows), :]), inner, ((1,), (0,)))
        for piece in range(pieces):
            item = items[step * pieces + piece]
            part = whole[piece * part_rows : (piece + 1) * part_rows]
            for col in range(order // LANES):
                item[col * part_rows : (col + 1) * part_rows, :] = part[
                    :, col * LANES : (col + 1) * LANES
                ]
            item[order // LANES * part_rows :, :] = target


def slots_kernel(count, stride, sectors, relay, *refs):
    slots, items = refs[len(refs) - count :], refs[: len(refs) - count]
    lines = slots[0].shape[0]
    here = lax.axis_index("op")
    tags = [item[lines:, :] for item in items]
    wanted = [
        lax.rem(here + step * stride, sectors).astype(jnp.float32) for step in range(count)
    ]
    picks = [[tag == want for tag in tags] for want in wanted]

    @pl.loop(0, lines // TAG, unroll=4)
    def _(tile):
        at = pl.ds(pl.multiple_of(tile * TAG, TAG), TAG)
        values = [item[at, :] for item in items]
        totals = []
        for step in range(count):
            total = jnp.where(picks[step][0], values[0], 0.0)
            for pick, value in zip(picks[step][1:], values[1:]):
                total = total + jnp.where(pick, value, 0.0)
            totals.append(total)
        if relay:
            low = here < sectors // 2
            totals[1], totals[3] = (
                jnp.where(low, totals[1], totals[3]),
                jnp.where(low, totals[3], totals[1]),
            )
        for step in range(count):
            slots[step][at, :] = totals[step]


def owned_kernel(layer, deep, relay, pieces, facts, *refs):
    out, parts = refs[-1], refs[:-1]
    rows, order = out.shape[1:]
    rows //= pieces
    live_rows, live_columns = facts[:1, :], facts[TAG : TAG + 1, :]
    depth = lax.axis_index("op") // layer
    edge = (depth == 0) | (depth == deep - 1)
    each = len(parts) // pieces
    for piece in range(pieces):
        first = lax.axis_index("term") * rows * pieces + piece * rows
        spot = first + lax.broadcasted_iota(jnp.int32, (rows, LANES), 0)
        across = lax.broadcasted_iota(jnp.int32, (rows, LANES), 1)
        own = parts[piece * each : (piece + 1) * each]
        for col in range(order // LANES):
            at = pl.ds(col * rows, rows)
            total = own[0][at, :] + own[1][at, :]
            if relay:
                total = total + jnp.where(edge, own[2][at, :], own[3][at, :] + own[4][at, :])
            else:
                for part in own[2:]:
                    total = total + part[at, :]
            live = (spot < live_rows) & (across + col * LANES < live_columns)
            out[0, pl.ds(piece * rows, rows), col * LANES : (col + 1) * LANES] = jnp.where(
                live, total, 0.0
            )


def on_device(sizes, wavefunction, left_dims, right_dims, left_operators, right_operators, charges):
    sectors, terms, deep, wide = sizes
    order = wavefunction.shape[1]
    rows = order // terms
    pieces = PIECES
    lines = order // LANES * rows // pieces
    layer = wide * CORES
    count = min(deep, (CHARGES - 1 + layer - 1) // layer + 1)
    relay = count == deep == 4
    depth = lax.axis_index("op") // layer
    edge = (depth == 0) | (depth == deep - 1)

    def shape(count):
        return jax.ShapeDtypeStruct((count, LANES), jnp.float32)

    def moved(value, dz, dx, dk):
        pairs = []
        for source in range(sectors):
            z, x, k = source // layer, source // CORES % wide, source % CORES
            z, x, k = (z + dz) % deep, (x + dx) % wide, (k + dk) % CORES
            pairs.append((source, (z * wide + x) * CORES + k))
        return lax.ppermute(value, "op", pairs)

    def along_line(value, hops):
        pairs = [
            (a * layer + rest, b * layer + rest) for a, b in hops.items() for rest in range(layer)
        ]
        return lax.ppermute(value, "op", pairs)

    def across_terms(value, step):
        return lax.ppermute(value, "term", [(t, (t + step) % terms) for t in range(terms)])

    def gathered(parts):
        own = [parts[0]] + [across_terms(parts[step], step) for step in range(1, terms)]
        plane = list(own)
        for step in range(1, wide):
            plane += [moved(item, 0, step, 0) for item in own]
        return plane + [moved(item, 0, 0, 1) for item in plane]

    def summed(items):
        slots = pl.pallas_call(
            functools.partial(slots_kernel, count, layer, sectors, relay),
            out_shape=[shape(lines)] * count,
            in_specs=[WHOLE] * len(items),
            out_specs=[WHOLE] * count,
            compiler_params=small(),
            name="slots",
        )(*items)
        if not relay:
            return [slots[0]] + [moved(slots[step], step, 0, 0) for step in range(1, count)]
        outer = along_line(slots[3], {0: 1, 1: 0, 2: 3, 3: 2})
        inner = along_line(slots[1], {1: 2, 2: 1, 0: 0, 3: 3})
        over = along_line(slots[2], {0: 2, 3: 1, 1: 0, 2: 3})
        last = along_line(
            jnp.where(edge, slots[1], slots[2] + outer), {0: 1, 3: 2, 1: 3, 2: 0}
        )
        return [slots[0], last, outer, inner, over]

    line = lax.broadcasted_iota(jnp.int32, (3 * TAG, LANES), 0)
    target = lax.rem(lax.axis_index("op") + charges[0, 0], sectors)
    facts = jnp.where(
        line < TAG, left_dims[0], jnp.where(line < 2 * TAG, right_dims[0], target)
    )
    inputs = (wavefunction, left_operators, right_operators)
    parts = pl.pallas_call(
        functools.partial(contribution_kernel, terms, pieces),
        out_shape=[shape(lines + TAG)] * (terms * pieces),
        in_specs=[WHOLE] + [HBM] * 3,
        out_specs=[WHOLE] * (terms * pieces),
        scratch_shapes=[pltpu.VMEM((order, order), jnp.float32)] * 3
        + [pltpu.SemaphoreType.DMA((3,))],
        compiler_params=small(),
        name="contribution",
    )(facts, *(pltpu.with_memory_space_constraint(value, pltpu.HBM) for value in inputs))
    sums = []
    for piece in range(pieces):
        sums += summed(gathered(parts[piece::pieces]))
    return pl.pallas_call(
        functools.partial(owned_kernel, layer, deep, relay, pieces),
        out_shape=jax.ShapeDtypeStruct((1, rows, order), jnp.float32),
        in_specs=[WHOLE] * (len(sums) + 1),
        out_specs=WHOLE,
        compiler_params=small(),
        name="owned",
    )(facts, *sums)


def factors(sectors):
    chips = sectors // CORES
    deep = 1
    while deep * deep < chips:
        deep *= 2
    return deep, chips // deep


def solution(mesh):
    sectors, terms = mesh.shape["op"], mesh.shape["term"]
    in_specs = (
        P("op", None, None),
        P("op"),
        P("op"),
        P("op", "term", None, None),
        P("op", "term", None, None),
        P("op", "term"),
    )
    return jax.shard_map(
        functools.partial(on_device, (sectors, terms, *factors(sectors))),
        mesh=mesh,
        in_specs=in_specs,
        out_specs=P("op", "term", None),
        check_vma=False,
    )
```

```python
import functools

import jax
import jax.numpy as jnp
from jax import lax
from jax.experimental import pallas as pl
from jax.experimental.pallas import tpu as pltpu
from jax.sharding import PartitionSpec as P

CHARGES = 12
LANES = 128
TAG = 8
CORES = 2
SHARES = (12, 12)
VMEM = 24 * 2**20


HBM = pl.BlockSpec(memory_space=pltpu.HBM)
WHOLE = pl.BlockSpec(memory_space=pltpu.VMEM)


def small():
    return pltpu.CompilerParams(vmem_limit_bytes=VMEM)


def halves(value):
    high = value.astype(jnp.bfloat16)
    return high, (value - high.astype(jnp.float32)).astype(jnp.bfloat16)


def product(left, right, dims):
    def one(a, b):
        return lax.dot_general(a, b, (dims, ((), ())), preferred_element_type=jnp.float32)

    depth, across = dims[0][0], dims[1][0]
    return one(
        jnp.concatenate([left[0], left[0], left[1]], axis=depth),
        jnp.concatenate([right[0], right[1], right[0]], axis=across),
    )


def contribution_kernel(terms, first, facts, wave, left, right, *refs):
    items = refs[:terms]
    wave_here, left_here, right_here, sems = refs[terms:]
    order = wave_here.shape[1]
    rows, height = order // terms, left_here.shape[0] // terms
    loads = [(wave.at[0], wave_here), (right.at[0, 0], right_here)]
    for step in range(terms):
        block = lax.rem(lax.axis_index("term") + step, terms)
        start = pl.multiple_of(block * rows + first, TAG)
        loads.append(
            (left.at[0, 0, pl.ds(start, height)], left_here.at[pl.ds(step * height, height)])
        )
    loads = [
        pltpu.make_async_copy(source, target, sems.at[index])
        for index, (source, target) in enumerate(loads)
    ]
    for load in loads:
        load.start()
    loads[0].wait()
    spot = lax.broadcasted_iota(jnp.int32, (order, LANES), 0)
    across = lax.broadcasted_iota(jnp.int32, (order, LANES), 1)
    live = jnp.concatenate(
        [
            (spot < facts[:1, :]) & (across + col < facts[TAG : TAG + 1, :])
            for col in range(0, order, LANES)
        ],
        axis=1,
    )
    masked = halves(jnp.where(live, wave_here[...], 0.0))
    for load in loads[2:]:
        load.wait()
    inner = halves(product(halves(left_here[...]), masked, ((1,), (0,))))
    loads[1].wait()
    whole = product(inner, halves(right_here[...]), ((1,), (1,)))
    target = facts[2 * TAG :, :].astype(jnp.float32)
    for step, item in enumerate(items):
        part = whole[step * height : (step + 1) * height]
        for col in range(order // LANES):
            item[col * height : (col + 1) * height, :] = part[
                :, col * LANES : (col + 1) * LANES
            ]
        item[order // LANES * height :, :] = target


def slots_kernel(count, stride, sectors, relay, *refs):
    slots, items = refs[len(refs) - count :], refs[: len(refs) - count]
    lines = slots[0].shape[0]
    here = lax.axis_index("op")
    tags = [item[lines:, :] for item in items]
    wanted = [
        lax.rem(here + step * stride, sectors).astype(jnp.float32) for step in range(count)
    ]
    picks = [[tag == want for tag in tags] for want in wanted]

    @pl.loop(0, lines // TAG, unroll=4)
    def _(tile):
        at = pl.ds(pl.multiple_of(tile * TAG, TAG), TAG)
        values = [item[at, :] for item in items]
        totals = []
        for step in range(count):
            total = jnp.where(picks[step][0], values[0], 0.0)
            for pick, value in zip(picks[step][1:], values[1:]):
                total = total + jnp.where(pick, value, 0.0)
            totals.append(total)
        if relay:
            low = here < sectors // 2
            totals[1], totals[3] = (
                jnp.where(low, totals[1], totals[3]),
                jnp.where(low, totals[3], totals[1]),
            )
        for step in range(count):
            slots[step][at, :] = totals[step]


def owned_kernel(layer, deep, relay, heights, facts, *refs):
    out, parts = refs[-1], refs[:-1]
    order = out.shape[2]
    live_rows, live_columns = facts[:1, :], facts[TAG : TAG + 1, :]
    depth = lax.axis_index("op") // layer
    edge = (depth == 0) | (depth == deep - 1)
    each = len(parts) // len(heights)
    for piece, rows in enumerate(heights):
        first = sum(heights[:piece])
        spot = lax.axis_index("term") * sum(heights) + first + lax.broadcasted_iota(jnp.int32, (rows, LANES), 0)
        across = lax.broadcasted_iota(jnp.int32, (rows, LANES), 1)
        own = parts[piece * each : (piece + 1) * each]
        for col in range(order // LANES):
            at = pl.ds(col * rows, rows)
            total = own[0][at, :] + own[1][at, :]
            if relay:
                total = total + jnp.where(edge, own[2][at, :], own[3][at, :] + own[4][at, :])
            else:
                for part in own[2:]:
                    total = total + part[at, :]
            live = (spot < live_rows) & (across + col * LANES < live_columns)
            out[0, pl.ds(first, rows), col * LANES : (col + 1) * LANES] = jnp.where(
                live, total, 0.0
            )


def on_device(sizes, wavefunction, left_dims, right_dims, left_operators, right_operators, charges):
    sectors, terms, deep, wide = sizes
    order = wavefunction.shape[1]
    rows = order // terms
    layer = wide * CORES
    count, relay = reach(deep, layer)
    heights = cut(rows) if relay else (rows,)
    pieces = len(heights)
    lines = [order // LANES * height for height in heights]
    depth = lax.axis_index("op") // layer
    edge = (depth == 0) | (depth == deep - 1)

    def shape(count):
        return jax.ShapeDtypeStruct((count, LANES), jnp.float32)

    def moved(value, dz, dx, dk):
        pairs = []
        for source in range(sectors):
            z, x, k = source // layer, source // CORES % wide, source % CORES
            z, x, k = (z + dz) % deep, (x + dx) % wide, (k + dk) % CORES
            pairs.append((source, (z * wide + x) * CORES + k))
        return lax.ppermute(value, "op", pairs)

    def along_line(value, hops):
        pairs = [
            (a * layer + rest, b * layer + rest) for a, b in hops.items() for rest in range(layer)
        ]
        return lax.ppermute(value, "op", pairs)

    def across_terms(value, step):
        return lax.ppermute(value, "term", [(t, (t + step) % terms) for t in range(terms)])

    def across_plane(value, dx, up):
        pairs = []
        for source in range(sectors):
            chip, k = source // CORES, source % CORES
            goal = (chip // wide * wide + (chip + dx) % wide) * CORES + k
            pairs += [
                (source * terms + t, goal * terms + (t + up) % terms) for t in range(terms)
            ]
        return lax.ppermute(value, ("op", "term"), pairs)

    def gathered(parts):
        own = [parts[0]]
        own += [across_terms(parts[step], step) for step in range(1, terms)]
        plane = list(own)
        for step in range(1, wide):
            plane.append(moved(parts[0], 0, step, 0))
            plane += [across_plane(parts[up], step, up) for up in range(1, terms)]
        return plane + [moved(item, 0, 0, 1) for item in plane]

    def summed(piece, items):
        slots = pl.pallas_call(
            functools.partial(slots_kernel, count, layer, sectors, relay),
            out_shape=[shape(lines[piece])] * count,
            in_specs=[WHOLE] * len(items),
            out_specs=[WHOLE] * count,
            compiler_params=small(),
            name="slots",
        )(*items)
        if not relay:
            return [slots[0]] + [moved(slots[step], step, 0, 0) for step in range(1, count)]
        outer = along_line(slots[3], {0: 1, 1: 0, 2: 3, 3: 2})
        inner = along_line(slots[1], {1: 2, 2: 1, 0: 0, 3: 3})
        over = along_line(slots[2], {0: 2, 3: 1, 1: 0, 2: 3})
        last = along_line(jnp.where(edge, slots[1], slots[2] + outer), {0: 1, 3: 2, 1: 3, 2: 0})
        return [slots[0], last, outer, inner, over]

    spot = lax.broadcasted_iota(jnp.int32, (3 * TAG, LANES), 0)
    target = lax.rem(lax.axis_index("op") + charges[0, 0], sectors)
    facts = jnp.where(
        spot < TAG, left_dims[0], jnp.where(spot < 2 * TAG, right_dims[0], target)
    )
    inputs = [
        pltpu.with_memory_space_constraint(value, pltpu.HBM)
        for value in (wavefunction, left_operators, right_operators)
    ]

    def contributed(piece):
        height = heights[piece]
        return pl.pallas_call(
            functools.partial(contribution_kernel, terms, sum(heights[:piece])),
            out_shape=[shape(lines[piece] + TAG)] * terms,
            in_specs=[WHOLE] + [HBM] * 3,
            out_specs=[WHOLE] * terms,
            scratch_shapes=[
                pltpu.VMEM((order, order), jnp.float32),
                pltpu.VMEM((terms * height, order), jnp.float32),
                pltpu.VMEM((order, order), jnp.float32),
                pltpu.SemaphoreType.DMA((2 + terms,)),
            ],
            compiler_params=small(),
            name="contribution",
        )(facts, *inputs)

    sums = []
    for piece in range(pieces):
        sums += summed(piece, gathered(contributed(piece)))
    return pl.pallas_call(
        functools.partial(owned_kernel, layer, deep, relay, heights),
        out_shape=jax.ShapeDtypeStruct((1, rows, order), jnp.float32),
        in_specs=[WHOLE] * (len(sums) + 1),
        out_specs=WHOLE,
        compiler_params=small(),
        name="owned",
    )(facts, *sums)


def factors(sectors):
    chips = sectors // CORES
    deep = 1
    while deep * deep < chips:
        deep *= 2
    return deep, chips // deep


def cut(rows):
    tiles = rows // TAG
    first = max(1, tiles * SHARES[0] // sum(SHARES))
    return first * TAG, rows - first * TAG


def reach(deep, layer):
    count = min(deep, (CHARGES - 1 + layer - 1) // layer + 1)
    return count, count == deep == 4


def solution(mesh):
    sectors, terms = mesh.shape["op"], mesh.shape["term"]
    deep, wide = factors(sectors)
    in_specs = (
        P("op", None, None),
        P("op"),
        P("op"),
        P("op", "term", None, None),
        P("op", "term", None, None),
        P("op", "term"),
    )

    def step(*args):
        return on_device((sectors, terms, deep, wide), *args)

    return jax.shard_map(
        step, mesh=mesh, in_specs=in_specs, out_specs=P("op", "term", None), check_vma=False
    )
```

```python
import functools

import jax
import jax.numpy as jnp
from jax import lax
from jax.experimental import pallas as pl
from jax.experimental.pallas import tpu as pltpu
from jax.sharding import PartitionSpec as P

CHARGES = 12
LANES = 128
TAG = 8
CORES = 2
SHARES = (12, 12)
VMEM = 24 * 2**20


HBM = pl.BlockSpec(memory_space=pltpu.HBM)
WHOLE = pl.BlockSpec(memory_space=pltpu.VMEM)


def small():
    return pltpu.CompilerParams(vmem_limit_bytes=VMEM)


def halves(value):
    high = value.astype(jnp.bfloat16)
    return high, (value - high.astype(jnp.float32)).astype(jnp.bfloat16)


def product(left, right, dims):
    def one(a, b):
        return lax.dot_general(a, b, (dims, ((), ())), preferred_element_type=jnp.float32)

    return one(left[0], right[0]) + (one(left[0], right[1]) + one(left[1], right[0]))


def contribution_kernel(terms, first, facts, wave, left, right, *refs):
    items = refs[:terms]
    wave_here, left_here, right_here, sems = refs[terms:]
    order = wave_here.shape[1]
    rows, height = order // terms, left_here.shape[0] // terms
    loads = [(wave.at[0], wave_here), (right.at[0, 0], right_here)]
    for step in range(terms):
        block = lax.rem(lax.axis_index("term") + step, terms)
        start = pl.multiple_of(block * rows + first, TAG)
        loads.append(
            (left.at[0, 0, pl.ds(start, height)], left_here.at[pl.ds(step * height, height)])
        )
    loads = [
        pltpu.make_async_copy(source, target, sems.at[index])
        for index, (source, target) in enumerate(loads)
    ]
    for load in loads:
        load.start()
    loads[0].wait()
    spot = lax.broadcasted_iota(jnp.int32, (order, LANES), 0)
    across = lax.broadcasted_iota(jnp.int32, (order, LANES), 1)
    live = jnp.concatenate(
        [
            (spot < facts[:1, :]) & (across + col < facts[TAG : TAG + 1, :])
            for col in range(0, order, LANES)
        ],
        axis=1,
    )
    masked = halves(jnp.where(live, wave_here[...], 0.0))
    for load in loads[2:]:
        load.wait()
    inner = halves(product(halves(left_here[...]), masked, ((1,), (0,))))
    loads[1].wait()
    whole = product(inner, halves(right_here[...]), ((1,), (1,)))
    target = facts[2 * TAG :, :].astype(jnp.float32)
    for step, item in enumerate(items):
        part = whole[step * height : (step + 1) * height]
        for col in range(order // LANES):
            item[col * height : (col + 1) * height, :] = part[
                :, col * LANES : (col + 1) * LANES
            ]
        item[order // LANES * height :, :] = target


def slots_kernel(count, stride, sectors, relay, *refs):
    slots, items = refs[len(refs) - count :], refs[: len(refs) - count]
    lines = slots[0].shape[0]
    here = lax.axis_index("op")
    tags = [item[lines:, :] for item in items]
    wanted = [
        lax.rem(here + step * stride, sectors).astype(jnp.float32) for step in range(count)
    ]
    picks = [[tag == want for tag in tags] for want in wanted]

    @pl.loop(0, lines // TAG, unroll=4)
    def _(tile):
        at = pl.ds(pl.multiple_of(tile * TAG, TAG), TAG)
        values = [item[at, :] for item in items]
        totals = []
        for step in range(count):
            total = jnp.where(picks[step][0], values[0], 0.0)
            for pick, value in zip(picks[step][1:], values[1:]):
                total = total + jnp.where(pick, value, 0.0)
            totals.append(total)
        if relay:
            low = here < sectors // 2
            totals[1], totals[3] = (
                jnp.where(low, totals[1], totals[3]),
                jnp.where(low, totals[3], totals[1]),
            )
        for step in range(count):
            slots[step][at, :] = totals[step]


def owned_kernel(layer, deep, relay, heights, facts, *refs):
    out, parts = refs[-1], refs[:-1]
    order = out.shape[2]
    live_rows, live_columns = facts[:1, :], facts[TAG : TAG + 1, :]
    depth = lax.axis_index("op") // layer
    edge = (depth == 0) | (depth == deep - 1)
    each = len(parts) // len(heights)
    for piece, rows in enumerate(heights):
        first = sum(heights[:piece])
        spot = lax.axis_index("term") * sum(heights) + first + lax.broadcasted_iota(jnp.int32, (rows, LANES), 0)
        across = lax.broadcasted_iota(jnp.int32, (rows, LANES), 1)
        own = parts[piece * each : (piece + 1) * each]
        for col in range(order // LANES):
            at = pl.ds(col * rows, rows)
            total = own[0][at, :] + own[1][at, :]
            if relay:
                total = total + jnp.where(edge, own[2][at, :], own[3][at, :] + own[4][at, :])
            else:
                for part in own[2:]:
                    total = total + part[at, :]
            live = (spot < live_rows) & (across + col * LANES < live_columns)
            out[0, pl.ds(first, rows), col * LANES : (col + 1) * LANES] = jnp.where(
                live, total, 0.0
            )


def on_device(sizes, wavefunction, left_dims, right_dims, left_operators, right_operators, charges):
    sectors, terms, deep, wide = sizes
    order = wavefunction.shape[1]
    rows = order // terms
    layer = wide * CORES
    count, relay = reach(deep, layer)
    heights = cut(rows) if relay else (rows,)
    pieces = len(heights)
    lines = [order // LANES * height for height in heights]
    depth = lax.axis_index("op") // layer
    edge = (depth == 0) | (depth == deep - 1)

    def shape(count):
        return jax.ShapeDtypeStruct((count, LANES), jnp.float32)

    def moved(value, dz, dx, dk):
        pairs = []
        for source in range(sectors):
            z, x, k = source // layer, source // CORES % wide, source % CORES
            z, x, k = (z + dz) % deep, (x + dx) % wide, (k + dk) % CORES
            pairs.append((source, (z * wide + x) * CORES + k))
        return lax.ppermute(value, "op", pairs)

    def along_line(value, hops):
        pairs = [
            (a * layer + rest, b * layer + rest) for a, b in hops.items() for rest in range(layer)
        ]
        return lax.ppermute(value, "op", pairs)

    def across_terms(value, step):
        return lax.ppermute(value, "term", [(t, (t + step) % terms) for t in range(terms)])

    def across_plane(value, dx, up):
        pairs = []
        for source in range(sectors):
            chip, k = source // CORES, source % CORES
            goal = (chip // wide * wide + (chip + dx) % wide) * CORES + k
            pairs += [
                (source * terms + t, goal * terms + (t + up) % terms) for t in range(terms)
            ]
        return lax.ppermute(value, ("op", "term"), pairs)

    def gathered(parts):
        own = [parts[0]]
        own += [across_terms(parts[step], step) for step in range(1, terms)]
        plane = list(own)
        for step in range(1, wide):
            plane.append(moved(parts[0], 0, step, 0))
            plane += [across_plane(parts[up], step, up) for up in range(1, terms)]
        return plane + [moved(item, 0, 0, 1) for item in plane]

    def summed(piece, items):
        slots = pl.pallas_call(
            functools.partial(slots_kernel, count, layer, sectors, relay),
            out_shape=[shape(lines[piece])] * count,
            in_specs=[WHOLE] * len(items),
            out_specs=[WHOLE] * count,
            compiler_params=small(),
            name="slots",
        )(*items)
        if not relay:
            return [slots[0]] + [moved(slots[step], step, 0, 0) for step in range(1, count)]
        outer = along_line(slots[3], {0: 1, 1: 0, 2: 3, 3: 2})
        inner = along_line(slots[1], {1: 2, 2: 1, 0: 0, 3: 3})
        over = along_line(slots[2], {0: 2, 3: 1, 1: 0, 2: 3})
        last = along_line(jnp.where(edge, slots[1], slots[2] + outer), {0: 1, 3: 2, 1: 3, 2: 0})
        return [slots[0], last, outer, inner, over]

    spot = lax.broadcasted_iota(jnp.int32, (3 * TAG, LANES), 0)
    target = lax.rem(lax.axis_index("op") + charges[0, 0], sectors)
    facts = jnp.where(
        spot < TAG, left_dims[0], jnp.where(spot < 2 * TAG, right_dims[0], target)
    )
    inputs = [
        pltpu.with_memory_space_constraint(value, pltpu.HBM)
        for value in (wavefunction, left_operators, right_operators)
    ]

    def contributed(piece):
        height = heights[piece]
        return pl.pallas_call(
            functools.partial(contribution_kernel, terms, sum(heights[:piece])),
            out_shape=[shape(lines[piece] + TAG)] * terms,
            in_specs=[WHOLE] + [HBM] * 3,
            out_specs=[WHOLE] * terms,
            scratch_shapes=[
                pltpu.VMEM((order, order), jnp.float32),
                pltpu.VMEM((terms * height, order), jnp.float32),
                pltpu.VMEM((order, order), jnp.float32),
                pltpu.SemaphoreType.DMA((2 + terms,)),
            ],
            compiler_params=small(),
            name="contribution",
        )(facts, *inputs)

    sums = []
    for piece in range(pieces):
        sums += summed(piece, gathered(contributed(piece)))
    return pl.pallas_call(
        functools.partial(owned_kernel, layer, deep, relay, heights),
        out_shape=jax.ShapeDtypeStruct((1, rows, order), jnp.float32),
        in_specs=[WHOLE] * (len(sums) + 1),
        out_specs=WHOLE,
        compiler_params=small(),
        name="owned",
    )(facts, *sums)


def factors(sectors):
    chips = sectors // CORES
    deep = 1
    while deep * deep < chips:
        deep *= 2
    return deep, chips // deep


def cut(rows):
    tiles = rows // TAG
    first = max(1, tiles * SHARES[0] // sum(SHARES))
    return first * TAG, rows - first * TAG


def reach(deep, layer):
    count = min(deep, (CHARGES - 1 + layer - 1) // layer + 1)
    return count, count == deep == 4


def solution(mesh):
    sectors, terms = mesh.shape["op"], mesh.shape["term"]
    deep, wide = factors(sectors)
    in_specs = (
        P("op", None, None),
        P("op"),
        P("op"),
        P("op", "term", None, None),
        P("op", "term", None, None),
        P("op", "term"),
    )

    def step(*args):
        return on_device((sectors, terms, deep, wide), *args)

    return jax.shard_map(
        step, mesh=mesh, in_specs=in_specs, out_specs=P("op", "term", None), check_vma=False
    )
```
